512 devices in a mesh: dp: 8 (over y, core), expert: 64 (over z, x).
Axes of the slice: x: 4, y: 4, z: 16, core: 2. Of those that a mesh axis runs over, the one named last changes fastest.
Arguments:
- tokens: bfloat16 [16384, 2048], P(('dp', 'expert')), may hold values from -6 to 6
- route_weight: float32 [16384, 8], P(('dp', 'expert')), may hold values from 0.03 to 0.4
- upstream: bfloat16 [16384, 2048], P(('dp', 'expert')), may hold values from -6 to 6
- expert_index: int32 [16384, 8], P(('dp', 'expert')), may hold values from 0 to 63, all different within a row; in each aligned block of 32 rows (0 to 31, 32 to 63, ...) at most 5 rows name the same one
- gate_weight: bfloat16 [64, 2048, 768], P('expert', 'dp'), may hold values from -0.125 to 0.125
- up_weight: bfloat16 [64, 2048, 768], P('expert', 'dp'), may hold values from -0.125 to 0.125
- down_weight: bfloat16 [64, 2048, 768], P('expert', 'dp'), may hold values from -0.21875 to 0.21875
Outputs:
- combined: bfloat16 [16384, 2048], P(('dp', 'expert'))
- token_grad: bfloat16 [16384, 2048], P(('dp', 'expert'))
- route_grad: float32 [16384, 8], P(('dp', 'expert'))
- down_grad: bfloat16 [64, 2048, 768], P('expert', 'dp')
The draws below stay inside these ranges and needn't reach their ends.
Inputs may be any that keep to these rules, and one draw needn't show every extreme that they name: `expert_index`: each row names 8 different experts. Among the rows of one device no expert is named more than 5 times, and in every draw some device names some expert exactly 5 times.
All inputs are finite; a program needn't handle non-finite values.
Results may differ from the reference program's by a relative error of at most 0.017.
Values may be sent and summed in bfloat16 or wider, within the bound.
A program may use at most 128 MiB of HBM per device.

```python
import math
import jax
import jax.numpy as jnp
import numpy as np
from jax import lax

D = 2048
FF = 768
TOPK = 8
TOK_DEV = 32
EXPERTS = 64
TOKENS = 16384
CAP = 5
N_DP = 8
N_EXPERT = 64


def block_scale(stream_key, shape, cuts, least, top_value):
    gain, own = 1.0, jax.random.fold_in(stream_key, 6)
    for axis_at, blocks in cuts:
        steps = jnp.exp(jax.random.uniform(jax.random.fold_in(own, axis_at), (blocks,), jnp.float32, least / len(cuts), top_value / len(cuts)))
        gain = gain * jnp.repeat(steps, shape[axis_at] // blocks).reshape([-1 if axis == axis_at else 1 for axis in range(len(shape))])
    return gain


def shared_out(own_key, own, number, rows, number_of, top, limit, skew):
    ranking = jax.random.permutation(own_key, number_of)
    heavy_load, common = shares(number_of, rows * top, limit, skew, True), shares(number_of, rows * top, limit, skew, False)
    places = jnp.arange(number_of)

    def named(lengths, rotation):
        used = int((lengths > 0).sum())
        fixed = max(1, used // 4)
        passed = fixed + (places - fixed + rotation * (used - fixed)) % max(1, number_of - fixed)
        return jnp.zeros((number_of,), jnp.int32).at[ranking[jnp.where(places < fixed, places, passed)]].set(jnp.asarray(lengths, jnp.int32))

    lengths = jnp.where(number % 4 == 0, named(heavy_load, number // 4), named(common, number - number // 4 - 1))
    mixed = jax.random.permutation(jax.random.fold_in(own, 3), number_of)
    giver, taker = mixed[0:number_of // 2 * 2:2], mixed[1:number_of // 2 * 2:2]
    margin = jnp.minimum(lengths[giver] - 1, limit - lengths[taker]) // 2
    margin = jnp.where((giver == ranking[0]) | (taker == ranking[0]) | (lengths[taker] == 0), 0, jnp.maximum(margin, 0))
    passed = jax.random.randint(jax.random.fold_in(own, 4), (number_of // 2,), 0, 1 << 20) % (margin + 1)
    lengths = lengths.at[giver].add(-passed).at[taker].add(passed)
    members = jnp.searchsorted(jnp.cumsum(lengths), jnp.arange(rows * top), side="right").astype(jnp.int32)
    grid = members.reshape(top, rows).T
    grid = grid[jax.random.permutation(jax.random.fold_in(own, 1), rows)]
    rotation = jax.random.randint(jax.random.fold_in(own, 2), (rows, 1), 0, top)
    return jnp.take_along_axis(grid, (jnp.arange(top)[None, :] + rotation) % top, axis=1)


def shares(amount, total, reach, skew, full):
    loads = [(1 << 20) // math.isqrt(rank ** skew) + 1 for rank in range(1, amount + 1)]
    largest = reach if full else min(reach, max(-(-total // amount), total * loads[0] // sum(loads)))
    least = 1 if total - largest >= amount - 1 else 0
    given, rest = [largest] + [least] * (amount - 1), total - largest - least * (amount - 1)
    while rest > 0:
        free = [i for i in range(1, amount) if given[i] < largest] or [i for i in range(1, amount) if given[i] < reach]
        whole, budget = sum([loads[i] for i in free]), rest
        for i in free:
            addition = min(reach - given[i], max(1, budget * loads[i] // whole), rest)
            given[i] = given[i] + addition
            rest = rest - addition
    return np.array(given)


def centred(key, dims, width, bound, shards=(), held_as=jnp.bfloat16):
    level = block_scale(key, dims, shards, -0.22, 0.18) if shards else 1.0
    array = jax.random.normal(key, dims, jnp.float32) * width * level
    return jnp.minimum(jnp.maximum(array, -bound), bound).astype(held_as)


def setup_inputs(seed: int = 0) -> dict:
    key_of = jax.random.split(jax.random.key(seed), 8)
    tokens = centred(key_of[0], (TOKENS, D), 1.0, 6.0, ((0, 512),))
    route_weight = jnp.clip(jnp.exp(math.log(0.4) - 2.5902672 * jax.random.uniform(key_of[1], (TOKENS, TOPK), jnp.float32) ** block_scale(key_of[1], (TOKENS, TOPK), ((0, 512),), -0.2, 0.2)), 0.03, 0.4)
    upstream = centred(key_of[2], (TOKENS, D), 1.0, 6.0, ((0, 512),))
    expert_index_keys = jax.random.split(jax.random.fold_in(key_of[3], 1), TOKENS // TOK_DEV)
    expert_index_turns = jax.random.permutation(jax.random.fold_in(key_of[3], 3), TOKENS // TOK_DEV)
    expert_index = jax.vmap(lambda own, number: shared_out(jax.random.fold_in(key_of[3], 2), own, number, TOK_DEV, EXPERTS, TOPK, CAP, 2))(expert_index_keys, expert_index_turns).reshape((TOKENS, TOPK))
    gate_weight = centred(key_of[4], (EXPERTS, D, FF), D ** -0.5, 0.125, ((0, 64), (1, 8)))
    up_weight = centred(key_of[5], (EXPERTS, D, FF), D ** -0.5, 0.125, ((0, 64), (1, 8)))
    down_weight = centred(key_of[6], (EXPERTS, D, FF), FF ** -0.5, 0.21875, ((0, 64), (1, 8)))
    return {"tokens": tokens, "route_weight": route_weight, "upstream": upstream, "expert_index": expert_index, "gate_weight": gate_weight, "up_weight": up_weight, "down_weight": down_weight}


def silu_parts(gate_value):
    sigmoid_value = jax.nn.sigmoid(gate_value)
    return gate_value * sigmoid_value, sigmoid_value * (1.0 + gate_value * (1.0 - sigmoid_value))


def contract_last(left, right):
    return lax.dot_general(left, right, (((1,), (1,)), ((), ())), preferred_element_type=jnp.float32)


def slot_table(expert_index):
    devices_all = N_DP * N_EXPERT
    assignments = TOK_DEV * TOPK
    flat_ids = expert_index.reshape(devices_all, assignments).astype(jnp.int32)
    onehot = (flat_ids[:, :, None] == jnp.arange(EXPERTS, dtype=jnp.int32)[None, None, :]).astype(jnp.int32)
    earlier = jnp.cumsum(onehot, axis=1) - onehot
    slot_value = jnp.sum(earlier * onehot, axis=2).astype(jnp.int32)
    device_of = jnp.broadcast_to(jnp.arange(devices_all, dtype=jnp.int32)[:, None], (devices_all, assignments))
    flat_place = (device_of * assignments + jnp.arange(assignments, dtype=jnp.int32)[None, :]).astype(jnp.int32)
    slot_grid = jnp.full((EXPERTS, devices_all, CAP), -1, jnp.int32)
    slot_grid = slot_grid.at[flat_ids, device_of, slot_value].set(flat_place)
    return slot_grid.reshape(EXPERTS, devices_all * CAP)


def reference(tokens, route_weight, upstream, expert_index, gate_weight, up_weight, down_weight):
    slot_grid = slot_table(expert_index)
    flat_route = route_weight.reshape(-1)
    row_total = N_EXPERT * CAP

    def per_expert(running, inputs):
        out_sum, grad_sum, route_sum = running
        slot_index, w_gate, w_up, w_down = inputs
        filled = slot_index >= 0
        safe_index = jnp.maximum(slot_index, 0).astype(jnp.int32)
        token_of = (safe_index // TOPK).astype(jnp.int32)
        routed_tokens = jnp.where(filled[:, None], tokens[token_of], jnp.zeros((), jnp.bfloat16))
        weight_of = jnp.where(filled, flat_route[safe_index], jnp.float32(0.0))
        upstream_rows = upstream[token_of].astype(jnp.float32)
        routed_grads = jnp.where(filled[:, None], weight_of[:, None] * upstream_rows, jnp.float32(0.0)).astype(jnp.bfloat16)
        gate_value = jnp.dot(routed_tokens, w_gate, preferred_element_type=jnp.float32)
        up_value = jnp.dot(routed_tokens, w_up, preferred_element_type=jnp.float32)
        activated, slope_value = silu_parts(gate_value)
        hidden = (activated * up_value).astype(jnp.bfloat16)
        expert_out = contract_last(hidden, w_down).astype(jnp.bfloat16)
        out_float = expert_out.astype(jnp.float32)
        out_sum = out_sum.at[token_of].add(jnp.where(filled[:, None], weight_of[:, None] * out_float, jnp.float32(0.0)))
        route_terms = jnp.sum(out_float * upstream_rows, axis=1)
        route_sum = route_sum.at[safe_index].add(jnp.where(filled, route_terms, jnp.float32(0.0)))
        hidden_grad = jnp.dot(routed_grads, w_down, preferred_element_type=jnp.float32)
        gate_grad = (hidden_grad * up_value * slope_value).astype(jnp.bfloat16)
        up_grad = (hidden_grad * activated).astype(jnp.bfloat16)
        row_grad = (contract_last(gate_grad, w_gate) + contract_last(up_grad, w_up)).astype(jnp.bfloat16)
        grad_sum = grad_sum.at[token_of].add(jnp.where(filled[:, None], row_grad.astype(jnp.float32), jnp.float32(0.0)))
        grads_group = routed_grads.reshape(N_DP, row_total, D).astype(jnp.float32)
        hidden_group = hidden.reshape(N_DP, row_total, FF).astype(jnp.float32)
        group_part = jnp.einsum("grd,grf->gdf", grads_group, hidden_group).astype(jnp.bfloat16)
        group_part = lax.optimization_barrier(group_part)
        down_grad = jnp.sum(group_part.astype(jnp.float32), axis=0).astype(jnp.bfloat16)
        return (out_sum, grad_sum, route_sum), down_grad

    initial = (jnp.zeros((TOKENS, D), jnp.float32), jnp.zeros((TOKENS, D), jnp.float32), jnp.zeros((TOKENS * TOPK,), jnp.float32))
    finals, down_grad = lax.scan(per_expert, initial, (slot_grid, gate_weight, up_weight, down_weight))
    out_sum, grad_sum, route_sum = finals
    return out_sum.astype(jnp.bfloat16), grad_sum.astype(jnp.bfloat16), route_sum.reshape(TOKENS, TOPK), down_grad
```

```python
import jax
import jax.numpy as jnp
from jax import lax
from jax.sharding import PartitionSpec as P

NX = 4
TAIL = 128


def contract_last(left, right):
    return lax.dot_general(
        left, right, (((1,), (1,)), ((), ())), preferred_element_type=jnp.float32
    )


def contract_first(left, right):
    return lax.dot_general(
        left, right, (((0,), (0,)), ((), ())), preferred_element_type=jnp.float32
    )


def three_parts(value):
    high = lax.reduce_precision(value, 8, 7)
    rest = value - high
    middle = lax.reduce_precision(rest, 8, 7)
    low = rest - middle
    return [part.astype(jnp.bfloat16) for part in (high, middle, low)]


def tail_of(parts):
    columns = jnp.concatenate(parts, axis=1)
    return jnp.pad(columns, ((0, 0), (0, TAIL - columns.shape[1])))


def on_device(tokens, route_weight, upstream, expert_index, gate_weight, up_weight, down_weight):
    n_experts = lax.axis_size("expert")
    nz = n_experts // NX
    tok_count, top_count = expert_index.shape
    width = tokens.shape[1]
    capacity = max(2, (5 * tok_count * top_count + 4 * n_experts - 1) // (4 * n_experts))
    me = lax.axis_index("expert")
    z_groups = [[z * NX + x for z in range(nz)] for x in range(NX)]
    x_groups = [[z * NX + x for x in range(NX)] for z in range(nz)]

    payload = jnp.concatenate(
        [tokens, upstream,
         tail_of([expert_index.astype(jnp.bfloat16)] + three_parts(route_weight))],
        axis=1,
    )
    full = payload.shape[1]
    gathered = lax.all_gather(payload, "expert", axis=0, tiled=True, axis_index_groups=z_groups)
    w_gate = lax.all_gather(gate_weight, "dp", axis=1, tiled=True)[0]
    w_up = lax.all_gather(up_weight, "dp", axis=1, tiled=True)[0]
    w_down = lax.all_gather(down_weight, "dp", axis=1, tiled=True)[0]

    row_z = me // NX
    named = gathered[:, 2 * width:2 * width + top_count].astype(jnp.float32)
    named = named.reshape(nz, tok_count, top_count)
    experts = (row_z * NX + jnp.arange(NX, dtype=jnp.int32)).astype(jnp.float32)
    match = (named[None] == experts[:, None, None, None]).any(axis=3)
    match_f = match.astype(jnp.bfloat16)
    before = jnp.triu(jnp.ones((tok_count, tok_count), jnp.bfloat16), 1)
    rank = lax.dot_general(
        match_f, before, (((2,), (0,)), ((), ())), preferred_element_type=jnp.float32
    )
    slots = jnp.arange(capacity, dtype=jnp.float32)
    sel = (match[:, :, None, :] & (rank[:, :, None, :] == slots[None, None, :, None])).astype(
        jnp.bfloat16
    )
    rows = lax.dot_general(
        sel.transpose(1, 0, 2, 3).reshape(nz, NX * capacity, tok_count),
        gathered.reshape(nz, tok_count, full),
        (((2,), (1,)), ((0,), (0,))),
        preferred_element_type=jnp.float32,
    ).astype(jnp.bfloat16)
    rows = rows.reshape(nz, NX, capacity, full).transpose(1, 0, 2, 3)
    rows = rows.reshape(NX, nz * capacity, full)
    arrived = lax.all_to_all(
        rows, "expert", split_axis=0, concat_axis=0, tiled=True, axis_index_groups=x_groups
    ).reshape(NX * nz * capacity, full)

    routed_tokens = arrived[:, :width]
    routed_up = arrived[:, width:2 * width]
    tail = arrived[:, 2 * width:].astype(jnp.float32)
    place = tail[:, :top_count] == me.astype(jnp.float32)
    weights = (
        tail[:, top_count:2 * top_count]
        + tail[:, 2 * top_count:3 * top_count]
        + tail[:, 3 * top_count:4 * top_count]
    )
    weight = jnp.sum(jnp.where(place, weights, 0.0), axis=1, keepdims=True)

    gate_value = jnp.dot(routed_tokens, w_gate, preferred_element_type=jnp.float32)
    up_value = jnp.dot(routed_tokens, w_up, preferred_element_type=jnp.float32)
    sig = jax.nn.sigmoid(gate_value)
    activated = gate_value * sig
    slope = sig * (1.0 + gate_value * (1.0 - sig))
    hidden_f = activated * up_value
    hidden = hidden_f.astype(jnp.bfloat16)
    raw_grad = jnp.dot(routed_up, w_down, preferred_element_type=jnp.float32)
    route_value = jnp.sum(hidden.astype(jnp.float32) * raw_grad, axis=1, keepdims=True)
    hidden_grad = raw_grad * weight
    weighted_hidden = (hidden_f * weight).astype(jnp.bfloat16)
    gate_grad = (hidden_grad * up_value * slope).astype(jnp.bfloat16)
    up_grad = (hidden_grad * activated).astype(jnp.bfloat16)
    out_rows = contract_last(weighted_hidden, w_down).astype(jnp.bfloat16)
    row_grad = (contract_last(gate_grad, w_gate) + contract_last(up_grad, w_up)).astype(
        jnp.bfloat16
    )
    route_tail = tail_of(three_parts(jnp.where(place, route_value, 0.0)))
    back = jnp.concatenate([out_rows, row_grad, route_tail], axis=1)
    returned = lax.all_to_all(
        back.reshape(NX, nz * capacity, full),
        "expert", split_axis=0, concat_axis=0, tiled=True, axis_index_groups=x_groups,
    )
    down_grad = lax.psum_scatter(
        contract_first(routed_up, weighted_hidden).astype(jnp.bfloat16),
        "dp", scatter_dimension=0, tiled=True,
    )[None]
    returned = returned.reshape(NX, nz, capacity, full).transpose(1, 0, 2, 3)
    partial = lax.dot_general(
        sel.transpose(1, 3, 0, 2).reshape(nz, tok_count, NX * capacity),
        returned.reshape(nz, NX * capacity, full),
        (((2,), (1,)), ((0,), (0,))),
        preferred_element_type=jnp.float32,
    ).astype(jnp.bfloat16)
    summed = lax.psum_scatter(
        partial.reshape(nz * tok_count, full), "expert", scatter_dimension=0, tiled=True,
        axis_index_groups=z_groups,
    )
    combined = summed[:, :width]
    token_grad = summed[:, width:2 * width]
    last = summed[:, 2 * width:].astype(jnp.float32)
    route_grad = (
        last[:, :top_count] + last[:, top_count:2 * top_count] + last[:, 2 * top_count:3 * top_count]
    )
    return (combined, token_grad, route_grad, down_grad)


def solution(mesh):
    return jax.shard_map(
        on_device,
        mesh=mesh,
        in_specs=(
            P(("dp", "expert"), None),
            P(("dp", "expert"), None),
            P(("dp", "expert"), None),
            P(("dp", "expert"), None),
            P("expert", "dp", None),
            P("expert", "dp", None),
            P("expert", "dp", None),
        ),
        out_specs=(
            P(("dp", "expert"), None),
            P(("dp", "expert"), None),
            P(("dp", "expert"), None),
            P("expert", "dp", None),
        ),
        check_vma=False,
    )
```

```python
import functools
import jax
import jax.numpy as jnp
from jax import lax
from jax.experimental import pallas as pl
from jax.experimental.pallas import tpu as pltpu
from jax.sharding import PartitionSpec as P

NX = 4
NC = 2
TAIL = 128


MESH = pl.DeviceIdType.MESH


def ring_ends(nz):
    me = lax.axis_index("expert")
    z, x = me // NX, me % NX
    right = lax.rem(z + 1, nz) * NX + x
    left = lax.rem(z + nz - 1, nz) * NX + x
    return z, ({"expert": right}, {"expert": left})


def greet(others):
    barrier = pltpu.get_barrier_semaphore()
    for other in others:
        pl.semaphore_signal(barrier, inc=1, device_id=other, device_id_type=MESH)
    pl.semaphore_wait(barrier, len(others))


def gather_kernel(
    nz, ny, own_ref, w0_ref, w1_ref, w2_ref, out_ref, g0_ref, g1_ref, g2_ref,
    local_sem, send_sem, recv_sem, wsend_sem, wrecv_sem,
):
    z, ends = ring_ends(nz)
    dp = lax.axis_index("dp")
    y, core = dp // NC, dp % NC
    behind = (lax.rem(y + ny - 1, ny) * NC + core, lax.rem(y + 1, ny) * NC + core)
    across = lax.rem(y + 2, ny) * NC + core
    ahead = ({"dp": behind[1]}, {"dp": behind[0]})
    sibling = {"dp": y * NC + 1 - core}
    greet(ends + ahead + (sibling,))
    half = nz // 2
    rows = own_ref.shape[0] // 2
    owned = (w0_ref, w1_ref, w2_ref)
    filled = (g0_ref, g1_ref, g2_ref)
    wrows = w0_ref.shape[0]

    def weight(j, k):
        own, full = owned[j], filled[j]
        if k < 2:
            source, target, to = own, full.at[dp], ahead[k]
        elif k < 4:
            part = pl.ds((k - 2) * (wrows // 2), wrows // 2)
            source = target = full.at[behind[k - 2], part]
            to = ahead[k - 2]
        elif k == 4:
            source, target, to = own, full.at[dp], sibling
        elif k < 7:
            source = target = full.at[behind[k - 5]]
            to = sibling
        else:
            part = pl.ds((k - 7) * (wrows // 2), wrows // 2)
            source = target = full.at[across, part]
            to = sibling
        return pltpu.make_async_remote_copy(
            src_ref=source, dst_ref=target,
            send_sem=wsend_sem.at[j, k], recv_sem=wrecv_sem.at[j, k],
            device_id=to, device_id_type=MESH,
        )

    def copy(step, way, chunk):
        block = lax.rem(z - step + nz, nz) if way == 0 else lax.rem(z + step, nz)
        part = pl.ds(chunk * rows, rows)
        source = own_ref.at[part] if step == 0 else out_ref.at[block, part]
        return pltpu.make_async_remote_copy(
            src_ref=source,
            dst_ref=out_ref.at[block, part],
            send_sem=send_sem.at[step, way, chunk],
            recv_sem=recv_sem.at[step, way, chunk],
            device_id=ends[way], device_id_type=MESH,
        )

    keep = [pltpu.make_async_copy(own_ref, out_ref.at[z], local_sem.at[3])] + [
        pltpu.make_async_copy(owned[j], filled[j].at[dp], local_sem.at[j]) for j in range(3)
    ]
    lanes = [(way, chunk) for chunk in range(2) for way in range(2)]
    for step in range(half):
        for way, chunk in lanes:
            if step > 0:
                copy(step - 1, way, chunk).wait_recv()
            if step < half - 1 or chunk == way:
                copy(step, way, chunk).start()
        if step == 0:
            for j in range(3):
                for k in (0, 1):
                    weight(j, k).start()
            for j in range(3):
                weight(j, 4).start()
            for one in keep:
                one.start()
        j = {2: 0, 4: 1, 5: 2}.get(step)
        if j is not None:
            for k in range(2):
                weight(j, k).wait_recv()
                weight(j, 2 + k).start()
                weight(j, 5 + k).start()
        if step == half - 1:
            for j in range(2):
                for k in range(2):
                    weight(j, 2 + k).wait_recv()
                    weight(j, 7 + k).start()
    for way in range(2):
        copy(half - 1, way, way).wait_recv()
    for k in range(2):
        weight(2, 2 + k).wait_recv()
        weight(2, 7 + k).start()
    for j in range(3):
        for k in range(4, 9):
            weight(j, k).wait_recv()
    for j in range(3):
        for k in range(9):
            weight(j, k).wait_send()
    for step in range(half):
        for way, chunk in lanes:
            if step < half - 1 or chunk == way:
                copy(step, way, chunk).wait_send()
    for one in keep:
        one.wait()


def ring_gather(payload, weights, nz, ny):
    rows, full = payload.shape
    half = nz // 2
    shards = [jax.ShapeDtypeStruct((ny * NC,) + w.shape, w.dtype) for w in weights]
    return pl.pallas_call(
        functools.partial(gather_kernel, nz, ny),
        out_shape=[jax.ShapeDtypeStruct((nz, rows, full), payload.dtype)] + shards,
        in_specs=[pl.BlockSpec(memory_space=pltpu.VMEM)] * 4,
        out_specs=[pl.BlockSpec(memory_space=pl.ANY)] * 4,
        scratch_shapes=[
            pltpu.SemaphoreType.DMA((4,)),
            pltpu.SemaphoreType.DMA((half, 2, 2)),
            pltpu.SemaphoreType.DMA((half, 2, 2)),
            pltpu.SemaphoreType.DMA((3, 9)),
            pltpu.SemaphoreType.DMA((3, 9)),
        ],
        compiler_params=pltpu.CompilerParams(collective_id=0, has_side_effects=True),
    )(payload, *weights)


def reduce_kernel(nz, part_ref, out_ref, held, going, send_sem, recv_sem):
    z, ends = ring_ends(nz)
    greet(ends)
    half = nz // 2
    rows = out_ref.shape[0] // 2

    def copy(step, way, chunk):
        return pltpu.make_async_remote_copy(
            src_ref=going.at[step, way, chunk],
            dst_ref=held.at[step, way, chunk],
            send_sem=send_sem.at[step, way, chunk],
            recv_sem=recv_sem.at[step, way, chunk],
            device_id=ends[way],
            device_id_type=pl.DeviceIdType.MESH,
        )

    def first(way, chunk):
        return 0 if chunk == way else 1

    lanes = [(way, chunk) for chunk in range(2) for way in range(2)]
    for step in range(half):
        for way, chunk in sorted(lanes, key=lambda lane: lane[0] != lane[1]):
            start = first(way, chunk)
            if step < start:
                continue
            distance = half - step
            block = lax.rem(z + distance, nz) if way == 0 else lax.rem(z - distance + nz, nz)
            value = part_ref[block, pl.ds(chunk * rows, rows), :]
            if step > start:
                copy(step - 1, way, chunk).wait_recv()
                value = (
                    value.astype(jnp.float32)
                    + held[step - 1, way, chunk].astype(jnp.float32)
                ).astype(value.dtype)
            going[step, way, chunk] = value
            copy(step, way, chunk).start()
    for chunk in range(2):
        total = part_ref[z, pl.ds(chunk * rows, rows), :].astype(jnp.float32)
        for way in range(2):
            copy(half - 1, way, chunk).wait_recv()
            total = total + held[half - 1, way, chunk].astype(jnp.float32)
        out_ref[pl.ds(chunk * rows, rows), :] = total.astype(out_ref.dtype)
    for step in range(half):
        for way, chunk in lanes:
            if step >= first(way, chunk):
                copy(step, way, chunk).wait_send()


def ring_reduce(partial):
    nz, rows, full = partial.shape
    half = nz // 2
    slots = (half, 2, 2, rows // 2, full)
    return pl.pallas_call(
        functools.partial(reduce_kernel, nz),
        out_shape=jax.ShapeDtypeStruct((rows, full), partial.dtype),
        in_specs=[pl.BlockSpec(memory_space=pltpu.VMEM)],
        out_specs=pl.BlockSpec(memory_space=pltpu.VMEM),
        scratch_shapes=[
            pltpu.VMEM(slots, partial.dtype),
            pltpu.VMEM(slots, partial.dtype),
            pltpu.SemaphoreType.DMA((half, 2, 2)),
            pltpu.SemaphoreType.DMA((half, 2, 2)),
        ],
        compiler_params=pltpu.CompilerParams(collective_id=1, has_side_effects=True),
        cost_estimate=pl.CostEstimate(
            flops=0, bytes_accessed=100_000_000, transcendentals=0
        ),
    )(partial)


def contract_last(left, right):
    return lax.dot_general(
        left, right, (((1,), (1,)), ((), ())), preferred_element_type=jnp.float32
    )


def contract_first(left, right):
    return lax.dot_general(
        left, right, (((0,), (0,)), ((), ())), preferred_element_type=jnp.float32
    )


def three_parts(value):
    high = lax.reduce_precision(value, 8, 7)
    rest = value - high
    middle = lax.reduce_precision(rest, 8, 7)
    low = rest - middle
    return [part.astype(jnp.bfloat16) for part in (high, middle, low)]


def tail_of(parts):
    columns = jnp.concatenate(parts, axis=1)
    return jnp.pad(columns, ((0, 0), (0, TAIL - columns.shape[1])))


def on_device(tokens, route_weight, upstream, expert_index, gate_weight, up_weight, down_weight):
    n_experts = lax.axis_size("expert")
    nz = n_experts // NX
    tok_count, top_count = expert_index.shape
    width = tokens.shape[1]
    capacity = max(2, (5 * tok_count * top_count + 4 * n_experts - 1) // (4 * n_experts))
    me = lax.axis_index("expert")
    n_dp = lax.axis_size("dp")
    ny = n_dp // NC
    x_groups = [[z * NX + x for x in range(NX)] for z in range(nz)]
    payload = jnp.concatenate(
        [tokens, upstream,
         tail_of([expert_index.astype(jnp.bfloat16)] + three_parts(route_weight))],
        axis=1,
    )
    full = payload.shape[1]
    gathered, *shards = ring_gather(
        payload, (gate_weight[0], up_weight[0], down_weight[0]), nz, ny
    )
    w_gate, w_up, w_down = (one.reshape(width, -1) for one in shards)

    row_z = me // NX
    named = gathered[:, :, 2 * width:2 * width + top_count].astype(jnp.float32)
    experts = (row_z * NX + jnp.arange(NX, dtype=jnp.int32)).astype(jnp.float32)
    match = (named[None] == experts[:, None, None, None]).any(axis=3)
    match_f = match.astype(jnp.bfloat16)
    before = jnp.triu(jnp.ones((tok_count, tok_count), jnp.bfloat16), 1)
    rank = lax.dot_general(
        match_f, before, (((2,), (0,)), ((), ())), preferred_element_type=jnp.float32
    )
    slots = jnp.arange(capacity, dtype=jnp.float32)
    sel = (match[:, :, None, :] & (rank[:, :, None, :] == slots[None, None, :, None])).astype(
        jnp.bfloat16
    )
    rows = lax.dot_general(
        sel.transpose(1, 0, 2, 3).reshape(nz, NX * capacity, tok_count),
        gathered,
        (((2,), (1,)), ((0,), (0,))),
        preferred_element_type=jnp.float32,
    ).astype(jnp.bfloat16)
    rows = rows.reshape(nz, NX, capacity, full).transpose(1, 0, 2, 3)
    rows = rows.reshape(NX, nz * capacity, full)
    arrived = lax.all_to_all(
        rows, "expert", split_axis=0, concat_axis=0, tiled=True, axis_index_groups=x_groups
    ).reshape(NX * nz * capacity, full)

    routed_tokens = arrived[:, :width]
    routed_up = arrived[:, width:2 * width]
    tail = arrived[:, 2 * width:].astype(jnp.float32)
    place = tail[:, :top_count] == me.astype(jnp.float32)
    weights = (
        tail[:, top_count:2 * top_count]
        + tail[:, 2 * top_count:3 * top_count]
        + tail[:, 3 * top_count:4 * top_count]
    )
    weight = jnp.sum(jnp.where(place, weights, 0.0), axis=1, keepdims=True)

    gate_value = jnp.dot(routed_tokens, w_gate, preferred_element_type=jnp.float32)
    up_value = jnp.dot(routed_tokens, w_up, preferred_element_type=jnp.float32)
    sig = jax.nn.sigmoid(gate_value)
    activated = gate_value * sig
    slope = sig * (1.0 + gate_value * (1.0 - sig))
    hidden_f = activated * up_value
    hidden = hidden_f.astype(jnp.bfloat16)
    raw_grad = jnp.dot(routed_up, w_down, preferred_element_type=jnp.float32)
    route_value = jnp.sum(hidden.astype(jnp.float32) * raw_grad, axis=1, keepdims=True)
    hidden_grad = raw_grad * weight
    weighted_hidden = (hidden_f * weight).astype(jnp.bfloat16)
    gate_grad = (hidden_grad * up_value * slope).astype(jnp.bfloat16)
    up_grad = (hidden_grad * activated).astype(jnp.bfloat16)
    out_rows = contract_last(weighted_hidden, w_down).astype(jnp.bfloat16)
    row_grad = (contract_last(gate_grad, w_gate) + contract_last(up_grad, w_up)).astype(
        jnp.bfloat16
    )
    route_tail = tail_of(three_parts(jnp.where(place, route_value, 0.0)))
    back = jnp.concatenate([out_rows, row_grad, route_tail], axis=1)
    returned = lax.all_to_all(
        back.reshape(NX, nz * capacity, full),
        "expert", split_axis=0, concat_axis=0, tiled=True, axis_index_groups=x_groups,
    )
    down_grad = lax.psum_scatter(
        contract_first(routed_up, weighted_hidden).astype(jnp.bfloat16),
        "dp", scatter_dimension=0, tiled=True,
    )[None]
    returned = returned.reshape(NX, nz, capacity, full).transpose(1, 0, 2, 3)
    partial = lax.dot_general(
        sel.transpose(1, 3, 0, 2).reshape(nz, tok_count, NX * capacity),
        returned.reshape(nz, NX * capacity, full),
        (((2,), (1,)), ((0,), (0,))),
        preferred_element_type=jnp.float32,
    ).astype(jnp.bfloat16)
    summed = ring_reduce(partial)
    combined = summed[:, :width]
    token_grad = summed[:, width:2 * width]
    last = summed[:, 2 * width:].astype(jnp.float32)
    route_grad = (
        last[:, :top_count] + last[:, top_count:2 * top_count] + last[:, 2 * top_count:3 * top_count]
    )
    return (combined, token_grad, route_grad, down_grad)


def solution(mesh):
    return jax.shard_map(
        on_device,
        mesh=mesh,
        in_specs=(
            P(("dp", "expert"), None),
            P(("dp", "expert"), None),
            P(("dp", "expert"), None),
            P(("dp", "expert"), None),
            P("expert", "dp", None),
            P("expert", "dp", None),
            P("expert", "dp", None),
        ),
        out_specs=(
            P(("dp", "expert"), None),
            P(("dp", "expert"), None),
            P(("dp", "expert"), None),
            P("expert", "dp", None),
        ),
        check_vma=False,
    )
```

```python
import functools
import jax
import jax.numpy as jnp
from jax import lax
from jax.experimental import pallas as pl
from jax.experimental.pallas import tpu as pltpu
from jax.sharding import PartitionSpec as P

NX = 4
NC = 2
TAIL = 128
SLOTS = 5
TILE = 16
BLOCK = 32
ORDER = (0, 1, -1, 2, -2, 3, -3, 4, -4, 5, -5, 6, -6, 7, -7, 8)
GROUP = 3
GROUPS = -(-len(ORDER) // GROUP)
COLUMNS = 384


MESH = pl.DeviceIdType.MESH


def contract_last(left, right):
    return lax.dot_general(
        left, right, (((1,), (1,)), ((), ())), preferred_element_type=jnp.float32
    )


def contract_first(left, right):
    return lax.dot_general(
        left, right, (((0,), (0,)), ((), ())), preferred_element_type=jnp.float32
    )


def three_parts(value):
    high = lax.reduce_precision(value, 8, 7)
    rest = value - high
    middle = lax.reduce_precision(rest, 8, 7)
    low = rest - middle
    return [part.astype(jnp.bfloat16) for part in (high, middle, low)]


def tail_of(parts):
    columns = jnp.concatenate(parts, axis=1)
    return jnp.pad(columns, ((0, 0), (0, TAIL - columns.shape[1])))


def ring_ends(nz):
    me = lax.axis_index("expert")
    z, x = me // NX, me % NX
    right = lax.rem(z + 1, nz) * NX + x
    left = lax.rem(z + nz - 1, nz) * NX + x
    return z, ({"expert": right}, {"expert": left})


def greet(others):
    barrier = pltpu.get_barrier_semaphore()
    for other in others:
        pl.semaphore_signal(barrier, inc=1, device_id=other, device_id_type=MESH)
    pl.semaphore_wait(barrier, len(others))


def x_peers():
    me = lax.axis_index("expert")
    z, x = me // NX, me % NX
    there = [lax.rem(x + step, NX) for step in range(1, NX)]
    return x, there, tuple({"expert": z * NX + other} for other in there)


def rows_of(distance, chunk):
    place = ORDER.index(8 if distance == -8 else distance)
    return pl.ds(place * BLOCK + chunk * TILE, TILE)


def group_rows(group):
    start = group * GROUP * BLOCK
    return pl.ds(start, min(GROUP * BLOCK, len(ORDER) * BLOCK - start))


def one_hots(tail, z, top_count):
    count = tail.shape[0]
    lanes = NX * TILE
    lane = lax.broadcasted_iota(jnp.int32, (count, lanes), 1)
    token = lax.broadcasted_iota(jnp.int32, (count, lanes), 0)
    expert = (z * NX + (lane >> 4)).astype(jnp.float32)
    match = jnp.zeros((count, lanes), jnp.float32)
    for k in range(top_count):
        match = jnp.where(tail[:, k:k + 1] == expert, 1.0, match)
    row = lax.broadcasted_iota(jnp.int32, (count, count), 0)
    col = lax.broadcasted_iota(jnp.int32, (count, count), 1)
    before = jnp.where(((row >> 5) == (col >> 5)) & (col < row), 1.0, 0.0)
    rank = jnp.dot(
        before.astype(jnp.bfloat16), match.astype(jnp.bfloat16),
        preferred_element_type=jnp.float32,
    )
    place = ((lane & (TILE - 1)) - SLOTS * (token >> 5)).astype(jnp.float32)
    return jnp.where(rank == place, match, 0.0).astype(jnp.bfloat16)


def gather_kernel(
    nz, ny, top_count, own_ref, w0_ref, w1_ref, w2_ref,
    out_ref, sel_ref, g0_ref, g1_ref, g2_ref,
    blocks, tiles, local_sem, send_sem, recv_sem, wsend_sem, wrecv_sem, xsend_sem, xrecv_sem,
):
    z, ends = ring_ends(nz)
    x, there, peers = x_peers()
    dp = lax.axis_index("dp")
    y, core = dp // NC, dp % NC
    behind = (lax.rem(y + ny - 1, ny) * NC + core, lax.rem(y + 1, ny) * NC + core)
    across = lax.rem(y + 2, ny) * NC + core
    ahead = ({"dp": behind[1]}, {"dp": behind[0]})
    sibling = {"dp": y * NC + 1 - core}
    greet(ends + ahead + (sibling,) + peers)
    half = nz // 2
    full_width = own_ref.shape[1]
    owned = (w0_ref, w1_ref, w2_ref)
    filled = (g0_ref, g1_ref, g2_ref)
    wrows = w0_ref.shape[0]

    def weight(j, k):
        own, full = owned[j], filled[j]
        if k < 2:
            source, target, to = own, full.at[dp], ahead[k]
        elif k < 4:
            part = pl.ds((k - 2) * (wrows // 2), wrows // 2)
            source = target = full.at[behind[k - 2], part]
            to = ahead[k - 2]
        elif k == 4:
            source, target, to = own, full.at[dp], sibling
        elif k < 7:
            source = target = full.at[behind[k - 5]]
            to = sibling
        else:
            part = pl.ds((k - 7) * (wrows // 2), wrows // 2)
            source = target = full.at[across, part]
            to = sibling
        return pltpu.make_async_remote_copy(
            src_ref=source, dst_ref=target,
            send_sem=wsend_sem.at[j, k], recv_sem=wrecv_sem.at[j, k],
            device_id=to, device_id_type=MESH,
        )

    def copy(step, way, chunk):
        sign = -1 if way == 0 else 1
        source = own_ref if step == 0 else blocks
        part = pl.ds(chunk * TILE, TILE) if step == 0 else rows_of(sign * step, chunk)
        return pltpu.make_async_remote_copy(
            src_ref=source.at[part],
            dst_ref=blocks.at[rows_of(sign * (step + 1), chunk)],
            send_sem=send_sem.at[step, way, chunk],
            recv_sem=recv_sem.at[step, way, chunk],
            device_id=ends[way], device_id_type=MESH,
        )

    def tile_copy(group, k):
        return pltpu.make_async_remote_copy(
            src_ref=tiles.at[group, there[k]],
            dst_ref=out_ref.at[x, pl.ds(group * TILE, TILE)],
            send_sem=xsend_sem.at[group, k], recv_sem=xrecv_sem.at[group, k],
            device_id=peers[k], device_id_type=MESH,
        )

    def tile_keep(group):
        return pltpu.make_async_copy(
            tiles.at[group, x], out_ref.at[x, pl.ds(group * TILE, TILE)],
            local_sem.at[3 + group],
        )

    def route(group):
        part = group_rows(group)
        tail = blocks[part, pl.ds(full_width - TAIL, TAIL)].astype(jnp.float32)
        sel = one_hots(tail, z, top_count)
        sel_ref[part, :] = sel

        def pick(i, carry):
            cut = pl.ds(pl.multiple_of(i * COLUMNS, 128), COLUMNS)
            picked = contract_first(sel, blocks[part, cut]).astype(jnp.bfloat16)
            tiles[group, :, :, cut] = picked.reshape(NX, TILE, COLUMNS)
            return carry

        lax.fori_loop(0, full_width // COLUMNS, pick, 0)
        for k in range(NX - 1):
            tile_copy(group, k).start()
        tile_keep(group).start()

    keep = [
        pltpu.make_async_copy(owned[j], filled[j].at[dp], local_sem.at[j]) for j in range(3)
    ]
    lanes = [(way, chunk) for chunk in range(2) for way in range(2)]
    for step in range(half):
        for way, chunk in lanes:
            if step > 0:
                copy(step - 1, way, chunk).wait_recv()
            if step < half - 1 or chunk == way:
                copy(step, way, chunk).start()
        if step == 0:
            for j in range(3):
                for k in (0, 1):
                    weight(j, k).start()
            for j in range(3):
                weight(j, 4).start()
            for one in keep:
                one.start()
            blocks[pl.ds(0, BLOCK), :] = own_ref[...]
        group = {1: 0, 3: 1, 4: 2, 6: 3, 7: 4}.get(step)
        if group is not None:
            route(group)
        j = {2: 0, 4: 1, 5: 2}.get(step)
        if j is not None:
            for k in range(2):
                weight(j, k).wait_recv()
                weight(j, 2 + k).start()
                weight(j, 5 + k).start()
        if step == half - 1:
            for j in range(2):
                for k in range(2):
                    weight(j, 2 + k).wait_recv()
                    weight(j, 7 + k).start()
    for way in range(2):
        copy(half - 1, way, way).wait_recv()
    route(GROUPS - 1)
    for k in range(2):
        weight(2, 2 + k).wait_recv()
        weight(2, 7 + k).start()
    for j in range(3):
        for k in range(4, 9):
            weight(j, k).wait_recv()
    for j in range(3):
        for k in range(9):
            weight(j, k).wait_send()
    for step in range(half):
        for way, chunk in lanes:
            if step < half - 1 or chunk == way:
                copy(step, way, chunk).wait_send()
    for group in range(GROUPS):
        for k in range(NX - 1):
            tile_copy(group, k).wait_recv()
            tile_copy(group, k).wait_send()
        tile_keep(group).wait()
    for one in keep:
        one.wait()


def ring_gather(payload, weights, nz, ny, top_count):
    rows, full = payload.shape
    half = nz // 2
    shards = [jax.ShapeDtypeStruct((ny * NC,) + w.shape, w.dtype) for w in weights]
    return pl.pallas_call(
        functools.partial(gather_kernel, nz, ny, top_count),
        out_shape=[
            jax.ShapeDtypeStruct((NX, GROUPS * TILE, full), payload.dtype),
            jax.ShapeDtypeStruct((nz * rows, NX * TILE), payload.dtype),
        ] + shards,
        in_specs=[pl.BlockSpec(memory_space=pltpu.VMEM)] * 4,
        out_specs=[
            pl.BlockSpec(memory_space=pl.ANY), pl.BlockSpec(memory_space=pltpu.VMEM)
        ] + [pl.BlockSpec(memory_space=pl.ANY)] * 3,
        scratch_shapes=[
            pltpu.VMEM((nz * rows, full), payload.dtype),
            pltpu.VMEM((GROUPS, NX, TILE, full), payload.dtype),
            pltpu.SemaphoreType.DMA((3 + GROUPS,)),
            pltpu.SemaphoreType.DMA((half, 2, 2)),
            pltpu.SemaphoreType.DMA((half, 2, 2)),
            pltpu.SemaphoreType.DMA((3, 9)),
            pltpu.SemaphoreType.DMA((3, 9)),
            pltpu.SemaphoreType.DMA((GROUPS, NX - 1)),
            pltpu.SemaphoreType.DMA((GROUPS, NX - 1)),
        ],
        compiler_params=pltpu.CompilerParams(collective_id=0, has_side_effects=True),
    )(payload, *weights)


def reduce_kernel(
    nz, back_ref, sel_ref, out_ref, landed, parts, held, going,
    local_sem, send_sem, recv_sem, xsend_sem, xrecv_sem,
):
    z, ends = ring_ends(nz)
    x, there, peers = x_peers()
    greet(ends + peers)
    half = nz // 2
    full_width = out_ref.shape[1]

    def tile_copy(group, k):
        return pltpu.make_async_remote_copy(
            src_ref=back_ref.at[there[k], pl.ds(group * TILE, TILE)],
            dst_ref=landed.at[group, x],
            send_sem=xsend_sem.at[group, k], recv_sem=xrecv_sem.at[group, k],
            device_id=peers[k], device_id_type=MESH,
        )

    def tile_keep(group):
        return pltpu.make_async_copy(
            back_ref.at[x, pl.ds(group * TILE, TILE)], landed.at[group, x],
            local_sem.at[group],
        )

    def add_up(group):
        for k in range(NX - 1):
            tile_copy(group, k).wait_recv()
        tile_keep(group).wait()
        part = group_rows(group)
        sel = sel_ref[part, :]

        def spread(i, carry):
            cut = pl.ds(pl.multiple_of(i * COLUMNS, 128), COLUMNS)
            rows = landed[group, :, :, cut].reshape(NX * TILE, COLUMNS)
            parts[part, cut] = jnp.dot(
                sel, rows, preferred_element_type=jnp.float32
            ).astype(jnp.bfloat16)
            return carry

        lax.fori_loop(0, full_width // COLUMNS, spread, 0)

    def copy(step, way, chunk):
        return pltpu.make_async_remote_copy(
            src_ref=going.at[step, way, chunk],
            dst_ref=held.at[step, way, chunk],
            send_sem=send_sem.at[step, way, chunk],
            recv_sem=recv_sem.at[step, way, chunk],
            device_id=ends[way], device_id_type=MESH,
        )

    def first(way, chunk):
        return 0 if chunk == way else 1

    for group in reversed(range(GROUPS)):
        for k in range(NX - 1):
            tile_copy(group, k).start()
        tile_keep(group).start()
    add_up(GROUPS - 1)
    lanes = [(way, chunk) for chunk in range(2) for way in range(2)]
    for step in range(half):
        for way, chunk in sorted(lanes, key=lambda lane: lane[0] != lane[1]):
            start = first(way, chunk)
            if step < start:
                continue
            distance = half - step
            value = parts[rows_of(distance if way == 0 else -distance, chunk), :]
            if step > start:
                copy(step - 1, way, chunk).wait_recv()
                value = (
                    value.astype(jnp.float32)
                    + held[step - 1, way, chunk].astype(jnp.float32)
                ).astype(value.dtype)
            going[step, way, chunk] = value
            copy(step, way, chunk).start()
        group = {0: 4, 1: 3, 3: 2, 4: 1, 6: 0}.get(step)
        if group is not None:
            add_up(group)
    for chunk in range(2):
        total = parts[rows_of(0, chunk), :].astype(jnp.float32)
        for way in range(2):
            copy(half - 1, way, chunk).wait_recv()
            total = total + held[half - 1, way, chunk].astype(jnp.float32)
        out_ref[pl.ds(chunk * TILE, TILE), :] = total.astype(out_ref.dtype)
    for step in range(half):
        for way, chunk in lanes:
            if step >= first(way, chunk):
                copy(step, way, chunk).wait_send()
    for group in range(GROUPS):
        for k in range(NX - 1):
            tile_copy(group, k).wait_send()


def ring_reduce(back, sel, nz):
    full = back.shape[2]
    rows = sel.shape[0] // nz
    half = nz // 2
    slots = (half, 2, 2, TILE, full)
    return pl.pallas_call(
        functools.partial(reduce_kernel, nz),
        out_shape=jax.ShapeDtypeStruct((rows, full), back.dtype),
        in_specs=[pl.BlockSpec(memory_space=pltpu.VMEM)] * 2,
        out_specs=pl.BlockSpec(memory_space=pltpu.VMEM),
        scratch_shapes=[
            pltpu.VMEM((GROUPS, NX, TILE, full), back.dtype),
            pltpu.VMEM((nz * rows, full), back.dtype),
            pltpu.VMEM(slots, back.dtype),
            pltpu.VMEM(slots, back.dtype),
            pltpu.SemaphoreType.DMA((GROUPS,)),
            pltpu.SemaphoreType.DMA((half, 2, 2)),
            pltpu.SemaphoreType.DMA((half, 2, 2)),
            pltpu.SemaphoreType.DMA((GROUPS, NX - 1)),
            pltpu.SemaphoreType.DMA((GROUPS, NX - 1)),
        ],
        compiler_params=pltpu.CompilerParams(collective_id=1, has_side_effects=True),
    )(back, sel)


def on_device(tokens, route_weight, upstream, expert_index, gate_weight, up_weight, down_weight):
    n_experts = lax.axis_size("expert")
    nz = n_experts // NX
    top_count = expert_index.shape[1]
    width = tokens.shape[1]
    me = lax.axis_index("expert")
    ny = lax.axis_size("dp") // NC
    payload = jnp.concatenate(
        [tokens, upstream,
         tail_of([expert_index.astype(jnp.bfloat16)] + three_parts(route_weight))],
        axis=1,
    )
    full = payload.shape[1]
    arrived, sel, *shards = ring_gather(
        payload, (gate_weight[0], up_weight[0], down_weight[0]), nz, ny, top_count
    )
    w_gate, w_up, w_down = (one.reshape(width, -1) for one in shards)
    arrived = arrived.reshape(NX * GROUPS * TILE, full)

    routed_tokens = arrived[:, :width]
    routed_up = arrived[:, width:2 * width]
    tail = arrived[:, 2 * width:].astype(jnp.float32)
    place = tail[:, :top_count] == me.astype(jnp.float32)
    weights = (
        tail[:, top_count:2 * top_count]
        + tail[:, 2 * top_count:3 * top_count]
        + tail[:, 3 * top_count:4 * top_count]
    )
    weight = jnp.sum(jnp.where(place, weights, 0.0), axis=1, keepdims=True)

    gate_value = jnp.dot(routed_tokens, w_gate, preferred_element_type=jnp.float32)
    up_value = jnp.dot(routed_tokens, w_up, preferred_element_type=jnp.float32)
    sig = jax.nn.sigmoid(gate_value)
    activated = gate_value * sig
    slope = sig * (1.0 + gate_value * (1.0 - sig))
    hidden_f = activated * up_value
    hidden = hidden_f.astype(jnp.bfloat16)
    raw_grad = jnp.dot(routed_up, w_down, preferred_element_type=jnp.float32)
    route_value = jnp.sum(hidden.astype(jnp.float32) * raw_grad, axis=1, keepdims=True)
    hidden_grad = raw_grad * weight
    weighted_hidden = (hidden_f * weight).astype(jnp.bfloat16)
    gate_grad = (hidden_grad * up_value * slope).astype(jnp.bfloat16)
    up_grad = (hidden_grad * activated).astype(jnp.bfloat16)
    out_rows = contract_last(weighted_hidden, w_down).astype(jnp.bfloat16)
    row_grad = (contract_last(gate_grad, w_gate) + contract_last(up_grad, w_up)).astype(
        jnp.bfloat16
    )
    route_tail = tail_of(three_parts(jnp.where(place, route_value, 0.0)))
    back = jnp.concatenate([out_rows, row_grad, route_tail], axis=1)
    down_grad = lax.psum_scatter(
        contract_first(routed_up, weighted_hidden).astype(jnp.bfloat16),
        "dp", scatter_dimension=0, tiled=True,
    )[None]
    summed = ring_reduce(back.reshape(NX, GROUPS * TILE, full), sel, nz)
    combined = summed[:, :width]
    token_grad = summed[:, width:2 * width]
    last = summed[:, 2 * width:].astype(jnp.float32)
    route_grad = (
        last[:, :top_count] + last[:, top_count:2 * top_count] + last[:, 2 * top_count:3 * top_count]
    )
    return (combined, token_grad, route_grad, down_grad)


def solution(mesh):
    return jax.shard_map(
        on_device,
        mesh=mesh,
        in_specs=(
            P(("dp", "expert"), None),
            P(("dp", "expert"), None),
            P(("dp", "expert"), None),
            P(("dp", "expert"), None),
            P("expert", "dp", None),
            P("expert", "dp", None),
            P("expert", "dp", None),
        ),
        out_specs=(
            P(("dp", "expert"), None),
            P(("dp", "expert"), None),
            P(("dp", "expert"), None),
            P("expert", "dp", None),
        ),
        check_vma=False,
    )
```

```python
import functools
import jax
import jax.numpy as jnp
from jax import lax
from jax.experimental import pallas as pl
from jax.experimental.pallas import tpu as pltpu
from jax.sharding import PartitionSpec as P

NX = 4
NC = 2
TAIL = 128
SLOTS = 5
TILE = 16
BLOCK = 32
ORDER = (0, 1, -1, 2, -2, 3, -3, 4, -4, 5, -5, 6, -6, 7, -7, 8)
GROUP = 3
GROUPS = -(-len(ORDER) // GROUP)
COLUMNS = 384


MESH = pl.DeviceIdType.MESH


def contract_last(left, right):
    return lax.dot_general(
        left, right, (((1,), (1,)), ((), ())), preferred_element_type=jnp.float32
    )


def contract_first(left, right):
    return lax.dot_general(
        left, right, (((0,), (0,)), ((), ())), preferred_element_type=jnp.float32
    )


def three_parts(value):
    high = lax.reduce_precision(value, 8, 7)
    rest = value - high
    middle = lax.reduce_precision(rest, 8, 7)
    low = rest - middle
    return [part.astype(jnp.bfloat16) for part in (high, middle, low)]


def tail_of(parts):
    columns = jnp.concatenate(parts, axis=1)
    return jnp.pad(columns, ((0, 0), (0, TAIL - columns.shape[1])))


def ring_ends(nz):
    me = lax.axis_index("expert")
    z, x = me // NX, me % NX
    right = lax.rem(z + 1, nz) * NX + x
    left = lax.rem(z + nz - 1, nz) * NX + x
    return z, ({"expert": right}, {"expert": left})


def greet(others):
    barrier = pltpu.get_barrier_semaphore()
    for other in others:
        pl.semaphore_signal(barrier, inc=1, device_id=other, device_id_type=MESH)
    pl.semaphore_wait(barrier, len(others))


def x_peers():
    me = lax.axis_index("expert")
    z, x = me // NX, me % NX
    there = [lax.rem(x + step, NX) for step in range(1, NX)]
    return x, there, tuple({"expert": z * NX + other} for other in there)


def dp_ends(ny):
    dp = lax.axis_index("dp")
    y, core = dp // NC, dp % NC
    behind = (lax.rem(y + ny - 1, ny) * NC + core, lax.rem(y + 1, ny) * NC + core)
    ahead = ({"dp": behind[1]}, {"dp": behind[0]})
    return dp, y, core, behind, ahead, {"dp": y * NC + 1 - core}


def rows_of(distance, chunk):
    place = ORDER.index(8 if distance == -8 else distance)
    return pl.ds(place * BLOCK + chunk * TILE, TILE)


def group_rows(group):
    start = group * GROUP * BLOCK
    return pl.ds(start, min(GROUP * BLOCK, len(ORDER) * BLOCK - start))


def one_hots(tail, z, top_count):
    count = tail.shape[0]
    lanes = NX * TILE
    lane = lax.broadcasted_iota(jnp.int32, (count, lanes), 1)
    token = lax.broadcasted_iota(jnp.int32, (count, lanes), 0)
    expert = (z * NX + (lane >> 4)).astype(jnp.float32)
    match = jnp.zeros((count, lanes), jnp.float32)
    for k in range(top_count):
        match = jnp.where(tail[:, k:k + 1] == expert, 1.0, match)
    row = lax.broadcasted_iota(jnp.int32, (count, count), 0)
    col = lax.broadcasted_iota(jnp.int32, (count, count), 1)
    before = jnp.where(((row >> 5) == (col >> 5)) & (col < row), 1.0, 0.0)
    rank = jnp.dot(
        before.astype(jnp.bfloat16), match.astype(jnp.bfloat16),
        preferred_element_type=jnp.float32,
    )
    place = ((lane & (TILE - 1)) - SLOTS * (token >> 5)).astype(jnp.float32)
    return jnp.where(rank == place, match, 0.0).astype(jnp.bfloat16)


def gather_kernel(
    nz, ny, top_count, own_ref, w0_ref, w1_ref, w2_ref,
    out_ref, sel_ref, g0_ref, g1_ref, g2_ref,
    blocks, tiles, local_sem, send_sem, recv_sem, wsend_sem, wrecv_sem, xsend_sem, xrecv_sem,
):
    z, ends = ring_ends(nz)
    x, there, peers = x_peers()
    dp, y, core, behind, ahead, sibling = dp_ends(ny)
    across = lax.rem(y + 2, ny) * NC + core
    greet(ends + ahead + (sibling,) + peers)
    half = nz // 2
    full_width = own_ref.shape[1]
    owned = (w0_ref, w1_ref, w2_ref)
    filled = (g0_ref, g1_ref, g2_ref)
    wrows = w0_ref.shape[0]

    def weight(j, k):
        own, full = owned[j], filled[j]
        if k < 2:
            source, target, to = own, full.at[dp], ahead[k]
        elif k < 4:
            part = pl.ds((k - 2) * (wrows // 2), wrows // 2)
            source = target = full.at[behind[k - 2], part]
            to = ahead[k - 2]
        elif k == 4:
            source, target, to = own, full.at[dp], sibling
        elif k < 7:
            source = target = full.at[behind[k - 5]]
            to = sibling
        else:
            part = pl.ds((k - 7) * (wrows // 2), wrows // 2)
            source = target = full.at[across, part]
            to = sibling
        return pltpu.make_async_remote_copy(
            src_ref=source, dst_ref=target,
            send_sem=wsend_sem.at[j, k], recv_sem=wrecv_sem.at[j, k],
            device_id=to, device_id_type=MESH,
        )

    def copy(step, way, chunk):
        sign = -1 if way == 0 else 1
        source = own_ref if step == 0 else blocks
        part = pl.ds(chunk * TILE, TILE) if step == 0 else rows_of(sign * step, chunk)
        return pltpu.make_async_remote_copy(
            src_ref=source.at[part],
            dst_ref=blocks.at[rows_of(sign * (step + 1), chunk)],
            send_sem=send_sem.at[step, way, chunk],
            recv_sem=recv_sem.at[step, way, chunk],
            device_id=ends[way], device_id_type=MESH,
        )

    def tile_copy(group, k):
        return pltpu.make_async_remote_copy(
            src_ref=tiles.at[group, there[k]],
            dst_ref=out_ref.at[x, pl.ds(group * TILE, TILE)],
            send_sem=xsend_sem.at[group, k], recv_sem=xrecv_sem.at[group, k],
            device_id=peers[k], device_id_type=MESH,
        )

    def tile_keep(group):
        return pltpu.make_async_copy(
            tiles.at[group, x], out_ref.at[x, pl.ds(group * TILE, TILE)],
            local_sem.at[3 + group],
        )

    def route(group):
        part = group_rows(group)
        tail = blocks[part, pl.ds(full_width - TAIL, TAIL)].astype(jnp.float32)
        sel = one_hots(tail, z, top_count)
        sel_ref[part, :] = sel

        def pick(i, carry):
            cut = pl.ds(pl.multiple_of(i * COLUMNS, 128), COLUMNS)
            picked = contract_first(sel, blocks[part, cut]).astype(jnp.bfloat16)
            tiles[group, :, :, cut] = picked.reshape(NX, TILE, COLUMNS)
            return carry

        lax.fori_loop(0, full_width // COLUMNS, pick, 0)
        for k in range(NX - 1):
            tile_copy(group, k).start()
        tile_keep(group).start()

    keep = [
        pltpu.make_async_copy(owned[j], filled[j].at[dp], local_sem.at[j]) for j in range(3)
    ]
    lanes = [(way, chunk) for chunk in range(2) for way in range(2)]
    for step in range(half):
        for way, chunk in lanes:
            if step > 0:
                copy(step - 1, way, chunk).wait_recv()
            if step < half - 1 or chunk == way:
                copy(step, way, chunk).start()
        if step == 0:
            for j in range(3):
                for k in (0, 1):
                    weight(j, k).start()
            for j in range(3):
                weight(j, 4).start()
            for one in keep:
                one.start()
            blocks[pl.ds(0, BLOCK), :] = own_ref[...]
        group = {1: 0, 3: 1, 4: 2, 6: 3, 7: 4}.get(step)
        if group is not None:
            route(group)
        j = {2: 0, 4: 1, 5: 2}.get(step)
        if j is not None:
            for k in range(2):
                weight(j, k).wait_recv()
                weight(j, 2 + k).start()
                weight(j, 5 + k).start()
        if step == half - 1:
            for j in range(2):
                for k in range(2):
                    weight(j, 2 + k).wait_recv()
                    weight(j, 7 + k).start()
    for way in range(2):
        copy(half - 1, way, way).wait_recv()
    route(GROUPS - 1)
    for k in range(2):
        weight(2, 2 + k).wait_recv()
        weight(2, 7 + k).start()
    for j in range(3):
        for k in range(4, 9):
            weight(j, k).wait_recv()
    for j in range(3):
        for k in range(9):
            weight(j, k).wait_send()
    for step in range(half):
        for way, chunk in lanes:
            if step < half - 1 or chunk == way:
                copy(step, way, chunk).wait_send()
    for group in range(GROUPS):
        for k in range(NX - 1):
            tile_copy(group, k).wait_recv()
            tile_copy(group, k).wait_send()
        tile_keep(group).wait()
    for one in keep:
        one.wait()


def ring_gather(payload, weights, nz, ny, top_count):
    rows, full = payload.shape
    half = nz // 2
    shards = [jax.ShapeDtypeStruct((ny * NC,) + w.shape, w.dtype) for w in weights]
    return pl.pallas_call(
        functools.partial(gather_kernel, nz, ny, top_count),
        out_shape=[
            jax.ShapeDtypeStruct((NX, GROUPS * TILE, full), payload.dtype),
            jax.ShapeDtypeStruct((nz * rows, NX * TILE), payload.dtype),
        ] + shards,
        in_specs=[pl.BlockSpec(memory_space=pltpu.VMEM)] * 4,
        out_specs=[
            pl.BlockSpec(memory_space=pl.ANY), pl.BlockSpec(memory_space=pltpu.VMEM)
        ] + [pl.BlockSpec(memory_space=pl.ANY)] * 3,
        scratch_shapes=[
            pltpu.VMEM((nz * rows, full), payload.dtype),
            pltpu.VMEM((GROUPS, NX, TILE, full), payload.dtype),
            pltpu.SemaphoreType.DMA((3 + GROUPS,)),
            pltpu.SemaphoreType.DMA((half, 2, 2)),
            pltpu.SemaphoreType.DMA((half, 2, 2)),
            pltpu.SemaphoreType.DMA((3, 9)),
            pltpu.SemaphoreType.DMA((3, 9)),
            pltpu.SemaphoreType.DMA((GROUPS, NX - 1)),
            pltpu.SemaphoreType.DMA((GROUPS, NX - 1)),
        ],
        compiler_params=pltpu.CompilerParams(collective_id=0, has_side_effects=True),
    )(payload, *weights)


def reduce_kernel(
    nz, ny, back_ref, sel_ref, down_ref, out_ref, grad_ref, landed, parts, held, going,
    paired, far, near, far_held, near_held,
    local_sem, send_sem, recv_sem, xsend_sem, xrecv_sem, dsend_sem, drecv_sem,
):
    z, ends = ring_ends(nz)
    x, there, peers = x_peers()
    dp, y, core, behind, ahead, sibling = dp_ends(ny)
    greet(ends + peers + ahead + (sibling,))
    half = nz // 2
    full_width = out_ref.shape[1]
    drows = grad_ref.shape[0] // 2

    def owner(turn, side):
        return lax.rem(y + turn, ny) * NC + side

    def down_copy(k):
        if k < ny:
            source, target, to = down_ref.at[owner(k, 1 - core)], paired.at[k], sibling
        elif k < ny + 2:
            way = k - ny
            source, target, to = far.at[way], far_held.at[way], ahead[way]
        else:
            way = k - ny - 2
            source, target, to = near.at[way], near_held.at[way], ahead[way]
        return pltpu.make_async_remote_copy(
            src_ref=source, dst_ref=target,
            send_sem=dsend_sem.at[k], recv_sem=drecv_sem.at[k],
            device_id=to, device_id_type=MESH,
        )

    def pair_sum(turn, piece):
        part = pl.ds(piece * TILE, TILE)
        return (
            down_ref[owner(turn, core), part, :].astype(jnp.float32)
            + paired[turn, part, :].astype(jnp.float32)
        )

    pieces = drows // TILE

    def down_far():
        down_copy(2).wait_recv()
        for way in range(2):
            def body(i, carry, way=way):
                far[way, pl.ds(i * TILE, TILE), :] = pair_sum(2, way * pieces + i).astype(far.dtype)
                return carry

            lax.fori_loop(0, pieces, body, 0)
            down_copy(ny + way).start()

    def down_near():
        for way, turn in ((0, 1), (1, 3)):
            down_copy(turn).wait_recv()
            down_copy(ny + way).wait_recv()

            def relayed(i, carry, way=way, turn=turn):
                part = pl.ds((way * pieces + i) * TILE, TILE)
                near[way, part, :] = (
                    pair_sum(turn, way * pieces + i)
                    + far_held[way, pl.ds(i * TILE, TILE), :].astype(jnp.float32)
                ).astype(near.dtype)
                return carry

            def plain(i, carry, way=way, turn=turn):
                at = (1 - way) * pieces + i
                near[way, pl.ds(at * TILE, TILE), :] = pair_sum(turn, at).astype(near.dtype)
                return carry

            lax.fori_loop(0, pieces, relayed, 0)
            lax.fori_loop(0, pieces, plain, 0)
            down_copy(ny + 2 + way).start()

    def down_last():
        down_copy(0).wait_recv()
        for way in range(2):
            down_copy(ny + 2 + way).wait_recv()

        def body(i, carry):
            part = pl.ds(i * TILE, TILE)
            total = pair_sum(0, i)
            for way in range(2):
                total = total + near_held[way, part, :].astype(jnp.float32)
            grad_ref[part, :] = total.astype(grad_ref.dtype)
            return carry

        lax.fori_loop(0, 2 * pieces, body, 0)

    def tile_copy(group, k):
        return pltpu.make_async_remote_copy(
            src_ref=back_ref.at[there[k], pl.ds(group * TILE, TILE)],
            dst_ref=landed.at[group, x],
            send_sem=xsend_sem.at[group, k], recv_sem=xrecv_sem.at[group, k],
            device_id=peers[k], device_id_type=MESH,
        )

    def tile_keep(group):
        return pltpu.make_async_copy(
            back_ref.at[x, pl.ds(group * TILE, TILE)], landed.at[group, x],
            local_sem.at[group],
        )

    def add_up(group):
        for k in range(NX - 1):
            tile_copy(group, k).wait_recv()
        tile_keep(group).wait()
        part = group_rows(group)
        sel = sel_ref[part, :]

        def spread(i, carry):
            cut = pl.ds(pl.multiple_of(i * COLUMNS, 128), COLUMNS)
            rows = landed[group, :, :, cut].reshape(NX * TILE, COLUMNS)
            parts[part, cut] = jnp.dot(
                sel, rows, preferred_element_type=jnp.float32
            ).astype(jnp.bfloat16)
            return carry

        lax.fori_loop(0, full_width // COLUMNS, spread, 0)

    def copy(step, way, chunk):
        return pltpu.make_async_remote_copy(
            src_ref=going.at[step, way, chunk],
            dst_ref=held.at[step, way, chunk],
            send_sem=send_sem.at[step, way, chunk],
            recv_sem=recv_sem.at[step, way, chunk],
            device_id=ends[way], device_id_type=MESH,
        )

    def first(way, chunk):
        return 0 if chunk == way else 1

    for group in reversed(range(GROUPS)):
        for k in range(NX - 1):
            tile_copy(group, k).start()
        tile_keep(group).start()
    for k in (2, 1, 3, 0):
        down_copy(k).start()
    down_far()
    add_up(GROUPS - 1)
    lanes = [(way, chunk) for chunk in range(2) for way in range(2)]
    for step in range(half):
        for way, chunk in sorted(lanes, key=lambda lane: lane[0] != lane[1]):
            start = first(way, chunk)
            if step < start:
                continue
            distance = half - step
            value = parts[rows_of(distance if way == 0 else -distance, chunk), :]
            if step > start:
                copy(step - 1, way, chunk).wait_recv()
                value = (
                    value.astype(jnp.float32)
                    + held[step - 1, way, chunk].astype(jnp.float32)
                ).astype(value.dtype)
            going[step, way, chunk] = value
            copy(step, way, chunk).start()
        group = {0: 4, 1: 3, 3: 2, 4: 1, 6: 0}.get(step)
        if group is not None:
            add_up(group)
        if step == 2:
            down_near()
        if step == 5:
            down_last()
    for chunk in range(2):
        total = parts[rows_of(0, chunk), :].astype(jnp.float32)
        for way in range(2):
            copy(half - 1, way, chunk).wait_recv()
            total = total + held[half - 1, way, chunk].astype(jnp.float32)
        out_ref[pl.ds(chunk * TILE, TILE), :] = total.astype(out_ref.dtype)
    for step in range(half):
        for way, chunk in lanes:
            if step >= first(way, chunk):
                copy(step, way, chunk).wait_send()
    for group in range(GROUPS):
        for k in range(NX - 1):
            tile_copy(group, k).wait_send()
    for k in range(ny + 4):
        down_copy(k).wait_send()


def ring_reduce(back, sel, down, nz, ny):
    full = back.shape[2]
    rows = sel.shape[0] // nz
    half = nz // 2
    slots = (half, 2, 2, TILE, full)
    drows, dcols = down.shape[1:]
    return pl.pallas_call(
        functools.partial(reduce_kernel, nz, ny),
        out_shape=[
            jax.ShapeDtypeStruct((rows, full), back.dtype),
            jax.ShapeDtypeStruct((drows, dcols), down.dtype),
        ],
        in_specs=[pl.BlockSpec(memory_space=pltpu.VMEM)] * 3,
        out_specs=[pl.BlockSpec(memory_space=pltpu.VMEM)] * 2,
        scratch_shapes=[
            pltpu.VMEM((GROUPS, NX, TILE, full), back.dtype),
            pltpu.VMEM((nz * rows, full), back.dtype),
            pltpu.VMEM(slots, back.dtype),
            pltpu.VMEM(slots, back.dtype),
            pltpu.VMEM((ny, drows, dcols), down.dtype),
            pltpu.VMEM((2, drows // 2, dcols), down.dtype),
            pltpu.VMEM((2, drows, dcols), down.dtype),
            pltpu.VMEM((2, drows // 2, dcols), down.dtype),
            pltpu.VMEM((2, drows, dcols), down.dtype),
            pltpu.SemaphoreType.DMA((GROUPS,)),
            pltpu.SemaphoreType.DMA((half, 2, 2)),
            pltpu.SemaphoreType.DMA((half, 2, 2)),
            pltpu.SemaphoreType.DMA((GROUPS, NX - 1)),
            pltpu.SemaphoreType.DMA((GROUPS, NX - 1)),
            pltpu.SemaphoreType.DMA((ny + 4,)),
            pltpu.SemaphoreType.DMA((ny + 4,)),
        ],
        compiler_params=pltpu.CompilerParams(collective_id=1, has_side_effects=True),
    )(back, sel, down)


def on_device(tokens, route_weight, upstream, expert_index, gate_weight, up_weight, down_weight):
    n_experts = lax.axis_size("expert")
    nz = n_experts // NX
    top_count = expert_index.shape[1]
    width = tokens.shape[1]
    me = lax.axis_index("expert")
    ny = lax.axis_size("dp") // NC
    payload = jnp.concatenate(
        [tokens, upstream,
         tail_of([expert_index.astype(jnp.bfloat16)] + three_parts(route_weight))],
        axis=1,
    )
    full = payload.shape[1]
    arrived, sel, *shards = ring_gather(
        payload, (gate_weight[0], up_weight[0], down_weight[0]), nz, ny, top_count
    )
    w_gate, w_up, w_down = (one.reshape(width, -1) for one in shards)
    arrived = arrived.reshape(NX * GROUPS * TILE, full)

    routed_tokens = arrived[:, :width]
    routed_up = arrived[:, width:2 * width]
    tail = arrived[:, 2 * width:].astype(jnp.float32)
    place = tail[:, :top_count] == me.astype(jnp.float32)
    weights = (
        tail[:, top_count:2 * top_count]
        + tail[:, 2 * top_count:3 * top_count]
        + tail[:, 3 * top_count:4 * top_count]
    )
    weight = jnp.sum(jnp.where(place, weights, 0.0), axis=1, keepdims=True)

    gate_value = jnp.dot(routed_tokens, w_gate, preferred_element_type=jnp.float32)
    up_value = jnp.dot(routed_tokens, w_up, preferred_element_type=jnp.float32)
    sig = jax.nn.sigmoid(gate_value)
    activated = gate_value * sig
    slope = sig * (1.0 + gate_value * (1.0 - sig))
    hidden_f = activated * up_value
    hidden = hidden_f.astype(jnp.bfloat16)
    raw_grad = jnp.dot(routed_up, w_down, preferred_element_type=jnp.float32)
    route_value = jnp.sum(hidden.astype(jnp.float32) * raw_grad, axis=1, keepdims=True)
    hidden_grad = raw_grad * weight
    weighted_hidden = (hidden_f * weight).astype(jnp.bfloat16)
    gate_grad = (hidden_grad * up_value * slope).astype(jnp.bfloat16)
    up_grad = (hidden_grad * activated).astype(jnp.bfloat16)
    out_rows = contract_last(weighted_hidden, w_down).astype(jnp.bfloat16)
    row_grad = (contract_last(gate_grad, w_gate) + contract_last(up_grad, w_up)).astype(
        jnp.bfloat16
    )
    route_tail = tail_of(three_parts(jnp.where(place, route_value, 0.0)))
    back = jnp.concatenate([out_rows, row_grad, route_tail], axis=1)
    down_part = contract_first(routed_up, weighted_hidden).astype(jnp.bfloat16)
    summed, down_grad = ring_reduce(
        back.reshape(NX, GROUPS * TILE, full), sel,
        down_part.reshape(ny * NC, -1, down_part.shape[1]), nz, ny,
    )
    combined = summed[:, :width]
    token_grad = summed[:, width:2 * width]
    last = summed[:, 2 * width:].astype(jnp.float32)
    route_grad = (
        last[:, :top_count] + last[:, top_count:2 * top_count] + last[:, 2 * top_count:3 * top_count]
    )
    return (combined, token_grad, route_grad, down_grad[None])


def solution(mesh):
    return jax.shard_map(
        on_device,
        mesh=mesh,
        in_specs=(
            P(("dp", "expert"), None),
            P(("dp", "expert"), None),
            P(("dp", "expert"), None),
            P(("dp", "expert"), None),
            P("expert", "dp", None),
            P("expert", "dp", None),
            P("expert", "dp", None),
        ),
        out_specs=(
            P(("dp", "expert"), None),
            P(("dp", "expert"), None),
            P(("dp", "expert"), None),
            P("expert", "dp", None),
        ),
        check_vma=False,
    )
```

```python
import functools
import jax
import jax.numpy as jnp
from jax import lax
from jax.experimental import pallas as pl
from jax.experimental.pallas import tpu as pltpu
from jax.sharding import PartitionSpec as P

NX = 4
NC = 2
TAIL = 128
SLOTS = 5
TILE = 16
BLOCK = 32
ORDER = (0, 1, -1, 2, -2, 3, -3, 4, -4, 5, -5, 6, -6, 7, -7, 8)
GROUP = 3
GROUPS = -(-len(ORDER) // GROUP)
COLUMNS = 384


MESH = pl.DeviceIdType.MESH


def contract_last(left, right):
    return lax.dot_general(
        left, right, (((1,), (1,)), ((), ())), preferred_element_type=jnp.float32
    )


def contract_first(left, right):
    return lax.dot_general(
        left, right, (((0,), (0,)), ((), ())), preferred_element_type=jnp.float32
    )


def three_parts(value):
    high = lax.reduce_precision(value, 8, 7)
    rest = value - high
    middle = lax.reduce_precision(rest, 8, 7)
    low = rest - middle
    return [part.astype(jnp.bfloat16) for part in (high, middle, low)]


def tail_of(parts):
    columns = jnp.concatenate(parts, axis=1)
    return jnp.pad(columns, ((0, 0), (0, TAIL - columns.shape[1])))


def ring_ends(nz):
    me = lax.axis_index("expert")
    z, x = me // NX, me % NX
    right = lax.rem(z + 1, nz) * NX + x
    left = lax.rem(z + nz - 1, nz) * NX + x
    return z, ({"expert": right}, {"expert": left})


def greet(others):
    barrier = pltpu.get_barrier_semaphore()
    for other in others:
        pl.semaphore_signal(barrier, inc=1, device_id=other, device_id_type=MESH)
    pl.semaphore_wait(barrier, len(others))


def x_peers():
    me = lax.axis_index("expert")
    z, x = me // NX, me % NX
    there = [lax.rem(x + step, NX) for step in range(1, NX)]
    return x, there, tuple({"expert": z * NX + other} for other in there)


def dp_ends(ny):
    dp = lax.axis_index("dp")
    y, core = dp // NC, dp % NC
    behind = (lax.rem(y + ny - 1, ny) * NC + core, lax.rem(y + 1, ny) * NC + core)
    ahead = ({"dp": behind[1]}, {"dp": behind[0]})
    return dp, y, core, behind, ahead, {"dp": y * NC + 1 - core}


def rows_of(distance, chunk):
    place = ORDER.index(8 if distance == -8 else distance)
    return pl.ds(place * BLOCK + chunk * TILE, TILE)


def group_rows(group):
    start = group * GROUP * BLOCK
    return pl.ds(start, min(GROUP * BLOCK, len(ORDER) * BLOCK - start))


def one_hots(tail, z, top_count):
    count = tail.shape[0]
    lanes = NX * TILE
    lane = lax.broadcasted_iota(jnp.int32, (count, lanes), 1)
    token = lax.broadcasted_iota(jnp.int32, (count, lanes), 0)
    expert = (z * NX + (lane >> 4)).astype(jnp.float32)
    match = jnp.zeros((count, lanes), jnp.float32)
    for k in range(top_count):
        match = jnp.where(tail[:, k:k + 1] == expert, 1.0, match)
    row = lax.broadcasted_iota(jnp.int32, (count, count), 0)
    col = lax.broadcasted_iota(jnp.int32, (count, count), 1)
    before = jnp.where(((row >> 5) == (col >> 5)) & (col < row), 1.0, 0.0)
    rank = jnp.dot(
        before.astype(jnp.bfloat16), match.astype(jnp.bfloat16),
        preferred_element_type=jnp.float32,
    )
    place = ((lane & (TILE - 1)) - SLOTS * (token >> 5)).astype(jnp.float32)
    return jnp.where(rank == place, match, 0.0).astype(jnp.bfloat16)


def gather_kernel(
    nz, ny, top_count, own_ref, w0_ref, w1_ref, w2_ref,
    out_ref, sel_ref, g0_ref, g1_ref, g2_ref,
    blocks, tiles, local_sem, send_sem, recv_sem, wsend_sem, wrecv_sem, xsend_sem, xrecv_sem,
):
    z, ends = ring_ends(nz)
    x, there, peers = x_peers()
    dp, y, core, behind, ahead, sibling = dp_ends(ny)
    across = lax.rem(y + 2, ny) * NC + core
    greet(ends + ahead + (sibling,) + peers)
    half = nz // 2
    full_width = own_ref.shape[1]
    owned = (w0_ref, w1_ref, w2_ref)
    filled = (g0_ref, g1_ref, g2_ref)
    wrows = w0_ref.shape[0]

    def weight(j, k):
        own, full = owned[j], filled[j]
        if k < 2:
            source, target, to = own, full.at[dp], ahead[k]
        elif k < 4:
            part = pl.ds((k - 2) * (wrows // 2), wrows // 2)
            source = target = full.at[behind[k - 2], part]
            to = ahead[k - 2]
        elif k == 4:
            source, target, to = own, full.at[dp], sibling
        elif k < 7:
            source = target = full.at[behind[k - 5]]
            to = sibling
        else:
            part = pl.ds((k - 7) * (wrows // 2), wrows // 2)
            source = target = full.at[across, part]
            to = sibling
        return pltpu.make_async_remote_copy(
            src_ref=source, dst_ref=target,
            send_sem=wsend_sem.at[j, k], recv_sem=wrecv_sem.at[j, k],
            device_id=to, device_id_type=MESH,
        )

    def copy(step, way, chunk):
        sign = -1 if way == 0 else 1
        source = own_ref if step == 0 else blocks
        part = pl.ds(chunk * TILE, TILE) if step == 0 else rows_of(sign * step, chunk)
        return pltpu.make_async_remote_copy(
            src_ref=source.at[part],
            dst_ref=blocks.at[rows_of(sign * (step + 1), chunk)],
            send_sem=send_sem.at[step, way, chunk],
            recv_sem=recv_sem.at[step, way, chunk],
            device_id=ends[way], device_id_type=MESH,
        )

    def tile_copy(group, k):
        return pltpu.make_async_remote_copy(
            src_ref=tiles.at[group, there[k]],
            dst_ref=out_ref.at[x, pl.ds(group * TILE, TILE)],
            send_sem=xsend_sem.at[group, k], recv_sem=xrecv_sem.at[group, k],
            device_id=peers[k], device_id_type=MESH,
        )

    def tile_keep(group):
        return pltpu.make_async_copy(
            tiles.at[group, x], out_ref.at[x, pl.ds(group * TILE, TILE)],
            local_sem.at[3 + group],
        )

    cuts = full_width // COLUMNS

    def route_first(group):
        part = group_rows(group)
        tail = blocks[part, pl.ds(full_width - TAIL, TAIL)].astype(jnp.float32)
        sel = one_hots(tail, z, top_count)
        sel_ref[part, :] = sel
        pick_rows(group, sel, 0, cuts // 2)

    def route_rest(group):
        pick_rows(group, sel_ref[group_rows(group), :], cuts // 2, cuts)
        for k in range(NX - 1):
            tile_copy(group, k).start()
        tile_keep(group).start()

    def pick_rows(group, sel, begin, end):
        part = group_rows(group)

        def pick(i, carry):
            cut = pl.ds(pl.multiple_of(i * COLUMNS, 128), COLUMNS)
            picked = contract_first(sel, blocks[part, cut]).astype(jnp.bfloat16)
            tiles[group, :, :, cut] = picked.reshape(NX, TILE, COLUMNS)
            return carry

        lax.fori_loop(begin, end, pick, 0)

    keep = [
        pltpu.make_async_copy(owned[j], filled[j].at[dp], local_sem.at[j]) for j in range(3)
    ]
    lanes = [(way, chunk) for chunk in range(2) for way in range(2)]
    begun = None
    for step in range(half):
        for way, chunk in lanes:
            if begun is not None and (way, chunk) == lanes[2]:
                route_rest(begun)
                begun = None
            if step > 0:
                copy(step - 1, way, chunk).wait_recv()
            if step < half - 1 or chunk == way:
                copy(step, way, chunk).start()
        if step == 0:
            for j in range(3):
                for k in (0, 1):
                    weight(j, k).start()
            for j in range(3):
                weight(j, 4).start()
            for one in keep:
                one.start()
            blocks[pl.ds(0, BLOCK), :] = own_ref[...]
        group = {1: 0, 3: 1, 4: 2, 6: 3, 7: 4}.get(step)
        if group is not None:
            route_first(group)
            begun = group
        j = {2: 0, 4: 1, 5: 2}.get(step)
        if j is not None:
            for k in range(2):
                weight(j, k).wait_recv()
                weight(j, 2 + k).start()
                weight(j, 5 + k).start()
        if step == half - 1:
            for j in range(2):
                for k in range(2):
                    weight(j, 2 + k).wait_recv()
                    weight(j, 7 + k).start()
    route_rest(begun)
    for way in range(2):
        copy(half - 1, way, way).wait_recv()
    route_first(GROUPS - 1)
    route_rest(GROUPS - 1)
    for k in range(2):
        weight(2, 2 + k).wait_recv()
        weight(2, 7 + k).start()
    for j in range(3):
        for k in range(4, 9):
            weight(j, k).wait_recv()
    for j in range(3):
        for k in range(9):
            weight(j, k).wait_send()
    for step in range(half):
        for way, chunk in lanes:
            if step < half - 1 or chunk == way:
                copy(step, way, chunk).wait_send()
    for group in range(GROUPS):
        for k in range(NX - 1):
            tile_copy(group, k).wait_recv()
            tile_copy(group, k).wait_send()
        tile_keep(group).wait()
    for one in keep:
        one.wait()


def ring_gather(payload, weights, nz, ny, top_count):
    rows, full = payload.shape
    half = nz // 2
    shards = [jax.ShapeDtypeStruct((ny * NC,) + w.shape, w.dtype) for w in weights]
    return pl.pallas_call(
        functools.partial(gather_kernel, nz, ny, top_count),
        out_shape=[
            jax.ShapeDtypeStruct((NX, GROUPS * TILE, full), payload.dtype),
            jax.ShapeDtypeStruct((nz * rows, NX * TILE), payload.dtype),
        ] + shards,
        in_specs=[pl.BlockSpec(memory_space=pltpu.VMEM)] * 4,
        out_specs=[
            pl.BlockSpec(memory_space=pl.ANY), pl.BlockSpec(memory_space=pltpu.VMEM)
        ] + [pl.BlockSpec(memory_space=pl.ANY)] * 3,
        scratch_shapes=[
            pltpu.VMEM((nz * rows, full), payload.dtype),
            pltpu.VMEM((GROUPS, NX, TILE, full), payload.dtype),
            pltpu.SemaphoreType.DMA((3 + GROUPS,)),
            pltpu.SemaphoreType.DMA((half, 2, 2)),
            pltpu.SemaphoreType.DMA((half, 2, 2)),
            pltpu.SemaphoreType.DMA((3, 9)),
            pltpu.SemaphoreType.DMA((3, 9)),
            pltpu.SemaphoreType.DMA((GROUPS, NX - 1)),
            pltpu.SemaphoreType.DMA((GROUPS, NX - 1)),
        ],
        compiler_params=pltpu.CompilerParams(collective_id=0, has_side_effects=True),
    )(payload, *weights)


def reduce_kernel(
    nz, ny, back_ref, sel_ref, down_ref, out_ref, grad_ref, landed, parts, held, going,
    paired, far, near, far_held, near_held,
    local_sem, send_sem, recv_sem, xsend_sem, xrecv_sem, dsend_sem, drecv_sem,
):
    z, ends = ring_ends(nz)
    x, there, peers = x_peers()
    dp, y, core, behind, ahead, sibling = dp_ends(ny)
    greet(ends + peers + ahead + (sibling,))
    half = nz // 2
    full_width = out_ref.shape[1]
    drows = grad_ref.shape[0] // 2

    def owner(turn, side):
        return lax.rem(y + turn, ny) * NC + side

    def down_copy(k):
        if k < ny:
            source, target, to = down_ref.at[owner(k, 1 - core)], paired.at[k], sibling
        elif k < ny + 2:
            way = k - ny
            source, target, to = far.at[way], far_held.at[way], ahead[way]
        else:
            way = k - ny - 2
            source, target, to = near.at[way], near_held.at[way], ahead[way]
        return pltpu.make_async_remote_copy(
            src_ref=source, dst_ref=target,
            send_sem=dsend_sem.at[k], recv_sem=drecv_sem.at[k],
            device_id=to, device_id_type=MESH,
        )

    def pair_sum(turn, piece):
        part = pl.ds(piece * TILE, TILE)
        return (
            down_ref[owner(turn, core), part, :].astype(jnp.float32)
            + paired[turn, part, :].astype(jnp.float32)
        )

    pieces = drows // TILE

    def down_far():
        down_copy(2).wait_recv()
        for way in range(2):
            def body(i, carry, way=way):
                far[way, pl.ds(i * TILE, TILE), :] = pair_sum(2, way * pieces + i).astype(far.dtype)
                return carry

            lax.fori_loop(0, pieces, body, 0)
            down_copy(ny + way).start()

    def down_near():
        for way, turn in ((0, 1), (1, 3)):
            down_copy(turn).wait_recv()
            down_copy(ny + way).wait_recv()

            def relayed(i, carry, way=way, turn=turn):
                part = pl.ds((way * pieces + i) * TILE, TILE)
                near[way, part, :] = (
                    pair_sum(turn, way * pieces + i)
                    + far_held[way, pl.ds(i * TILE, TILE), :].astype(jnp.float32)
                ).astype(near.dtype)
                return carry

            def plain(i, carry, way=way, turn=turn):
                at = (1 - way) * pieces + i
                near[way, pl.ds(at * TILE, TILE), :] = pair_sum(turn, at).astype(near.dtype)
                return carry

            lax.fori_loop(0, pieces, relayed, 0)
            lax.fori_loop(0, pieces, plain, 0)
            down_copy(ny + 2 + way).start()

    def down_last():
        down_copy(0).wait_recv()
        for way in range(2):
            down_copy(ny + 2 + way).wait_recv()

        def body(i, carry):
            part = pl.ds(i * TILE, TILE)
            total = pair_sum(0, i)
            for way in range(2):
                total = total + near_held[way, part, :].astype(jnp.float32)
            grad_ref[part, :] = total.astype(grad_ref.dtype)
            return carry

        lax.fori_loop(0, 2 * pieces, body, 0)

    def tile_copy(group, k):
        return pltpu.make_async_remote_copy(
            src_ref=back_ref.at[there[k], pl.ds(group * TILE, TILE)],
            dst_ref=landed.at[group, x],
            send_sem=xsend_sem.at[group, k], recv_sem=xrecv_sem.at[group, k],
            device_id=peers[k], device_id_type=MESH,
        )

    def tile_keep(group):
        return pltpu.make_async_copy(
            back_ref.at[x, pl.ds(group * TILE, TILE)], landed.at[group, x],
            local_sem.at[group],
        )

    cuts = full_width // COLUMNS

    def add_up(group, begin=0, end=cuts):
        if begin == 0:
            for k in range(NX - 1):
                tile_copy(group, k).wait_recv()
            tile_keep(group).wait()
        part = group_rows(group)
        sel = sel_ref[part, :]

        def spread(i, carry):
            cut = pl.ds(pl.multiple_of(i * COLUMNS, 128), COLUMNS)
            rows = landed[group, :, :, cut].reshape(NX * TILE, COLUMNS)
            parts[part, cut] = jnp.dot(
                sel, rows, preferred_element_type=jnp.float32
            ).astype(jnp.bfloat16)
            return carry

        lax.fori_loop(begin, end, spread, 0)

    def copy(step, way, chunk):
        return pltpu.make_async_remote_copy(
            src_ref=going.at[step, way, chunk],
            dst_ref=held.at[step, way, chunk],
            send_sem=send_sem.at[step, way, chunk],
            recv_sem=recv_sem.at[step, way, chunk],
            device_id=ends[way], device_id_type=MESH,
        )

    def first(way, chunk):
        return 0 if chunk == way else 1

    for group in reversed(range(GROUPS)):
        for k in range(NX - 1):
            tile_copy(group, k).start()
        tile_keep(group).start()
    for k in (2, 1, 3, 0):
        down_copy(k).start()
    down_far()
    add_up(GROUPS - 1)
    lanes = [(way, chunk) for chunk in range(2) for way in range(2)]
    for step in range(half):
        for at, (way, chunk) in enumerate(sorted(lanes, key=lambda lane: lane[0] != lane[1])):
            start = first(way, chunk)
            if step < start:
                continue
            if at == 2 and step in (3, 4, 6):
                add_up({3: 2, 4: 1, 6: 0}[step], 0, cuts // 2)
            distance = half - step
            value = parts[rows_of(distance if way == 0 else -distance, chunk), :]
            if step > start:
                copy(step - 1, way, chunk).wait_recv()
                value = (
                    value.astype(jnp.float32)
                    + held[step - 1, way, chunk].astype(jnp.float32)
                ).astype(value.dtype)
            going[step, way, chunk] = value
            copy(step, way, chunk).start()
        group = {0: 4, 1: 3, 3: 2, 4: 1, 6: 0}.get(step)
        if group is not None:
            add_up(group, 0 if step < 3 else cuts // 2)
        if step == 2:
            down_near()
        if step == 5:
            down_last()
    for chunk in range(2):
        total = parts[rows_of(0, chunk), :].astype(jnp.float32)
        for way in range(2):
            copy(half - 1, way, chunk).wait_recv()
            total = total + held[half - 1, way, chunk].astype(jnp.float32)
        out_ref[pl.ds(chunk * TILE, TILE), :] = total.astype(out_ref.dtype)
    for step in range(half):
        for way, chunk in lanes:
            if step >= first(way, chunk):
                copy(step, way, chunk).wait_send()
    for group in range(GROUPS):
        for k in range(NX - 1):
            tile_copy(group, k).wait_send()
    for k in range(ny + 4):
        down_copy(k).wait_send()


def ring_reduce(back, sel, down, nz, ny):
    full = back.shape[2]
    rows = sel.shape[0] // nz
    half = nz // 2
    slots = (half, 2, 2, TILE, full)
    drows, dcols = down.shape[1:]
    return pl.pallas_call(
        functools.partial(reduce_kernel, nz, ny),
        out_shape=[
            jax.ShapeDtypeStruct((rows, full), back.dtype),
            jax.ShapeDtypeStruct((drows, dcols), down.dtype),
        ],
        in_specs=[pl.BlockSpec(memory_space=pltpu.VMEM)] * 3,
        out_specs=[pl.BlockSpec(memory_space=pltpu.VMEM)] * 2,
        scratch_shapes=[
            pltpu.VMEM((GROUPS, NX, TILE, full), back.dtype),
            pltpu.VMEM((nz * rows, full), back.dtype),
            pltpu.VMEM(slots, back.dtype),
            pltpu.VMEM(slots, back.dtype),
            pltpu.VMEM((ny, drows, dcols), down.dtype),
            pltpu.VMEM((2, drows // 2, dcols), down.dtype),
            pltpu.VMEM((2, drows, dcols), down.dtype),
            pltpu.VMEM((2, drows // 2, dcols), down.dtype),
            pltpu.VMEM((2, drows, dcols), down.dtype),
            pltpu.SemaphoreType.DMA((GROUPS,)),
            pltpu.SemaphoreType.DMA((half, 2, 2)),
            pltpu.SemaphoreType.DMA((half, 2, 2)),
            pltpu.SemaphoreType.DMA((GROUPS, NX - 1)),
            pltpu.SemaphoreType.DMA((GROUPS, NX - 1)),
            pltpu.SemaphoreType.DMA((ny + 4,)),
            pltpu.SemaphoreType.DMA((ny + 4,)),
        ],
        compiler_params=pltpu.CompilerParams(collective_id=1, has_side_effects=True),
    )(back, sel, down)


def on_device(tokens, route_weight, upstream, expert_index, gate_weight, up_weight, down_weight):
    n_experts = lax.axis_size("expert")
    nz = n_experts // NX
    top_count = expert_index.shape[1]
    width = tokens.shape[1]
    me = lax.axis_index("expert")
    ny = lax.axis_size("dp") // NC
    payload = jnp.concatenate(
        [tokens, upstream,
         tail_of([expert_index.astype(jnp.bfloat16)] + three_parts(route_weight))],
        axis=1,
    )
    full = payload.shape[1]
    arrived, sel, *shards = ring_gather(
        payload, (gate_weight[0], up_weight[0], down_weight[0]), nz, ny, top_count
    )
    w_gate, w_up, w_down = (one.reshape(width, -1) for one in shards)
    arrived = arrived.reshape(NX * GROUPS * TILE, full)

    routed_tokens = arrived[:, :width]
    routed_up = arrived[:, width:2 * width]
    tail = arrived[:, 2 * width:].astype(jnp.float32)
    place = tail[:, :top_count] == me.astype(jnp.float32)
    weights = (
        tail[:, top_count:2 * top_count]
        + tail[:, 2 * top_count:3 * top_count]
        + tail[:, 3 * top_count:4 * top_count]
    )
    weight = jnp.sum(jnp.where(place, weights, 0.0), axis=1, keepdims=True)

    gate_value = jnp.dot(routed_tokens, w_gate, preferred_element_type=jnp.float32)
    up_value = jnp.dot(routed_tokens, w_up, preferred_element_type=jnp.float32)
    sig = jax.nn.sigmoid(gate_value)
    activated = gate_value * sig
    slope = sig * (1.0 + gate_value * (1.0 - sig))
    hidden_f = activated * up_value
    hidden = hidden_f.astype(jnp.bfloat16)
    raw_grad = jnp.dot(routed_up, w_down, preferred_element_type=jnp.float32)
    route_value = jnp.sum(hidden.astype(jnp.float32) * raw_grad, axis=1, keepdims=True)
    hidden_grad = raw_grad * weight
    weighted_hidden = (hidden_f * weight).astype(jnp.bfloat16)
    gate_grad = (hidden_grad * up_value * slope).astype(jnp.bfloat16)
    up_grad = (hidden_grad * activated).astype(jnp.bfloat16)
    out_rows = contract_last(weighted_hidden, w_down).astype(jnp.bfloat16)
    row_grad = (contract_last(gate_grad, w_gate) + contract_last(up_grad, w_up)).astype(
        jnp.bfloat16
    )
    route_tail = tail_of(three_parts(jnp.where(place, route_value, 0.0)))
    back = jnp.concatenate([out_rows, row_grad, route_tail], axis=1)
    down_part = contract_first(routed_up, weighted_hidden).astype(jnp.bfloat16)
    summed, down_grad = ring_reduce(
        back.reshape(NX, GROUPS * TILE, full), sel,
        down_part.reshape(ny * NC, -1, down_part.shape[1]), nz, ny,
    )
    combined = summed[:, :width]
    token_grad = summed[:, width:2 * width]
    last = summed[:, 2 * width:].astype(jnp.float32)
    route_grad = (
        last[:, :top_count] + last[:, top_count:2 * top_count] + last[:, 2 * top_count:3 * top_count]
    )
    return (combined, token_grad, route_grad, down_grad[None])


def solution(mesh):
    return jax.shard_map(
        on_device,
        mesh=mesh,
        in_specs=(
            P(("dp", "expert"), None),
            P(("dp", "expert"), None),
            P(("dp", "expert"), None),
            P(("dp", "expert"), None),
            P("expert", "dp", None),
            P("expert", "dp", None),
            P("expert", "dp", None),
        ),
        out_specs=(
            P(("dp", "expert"), None),
            P(("dp", "expert"), None),
            P(("dp", "expert"), None),
            P("expert", "dp", None),
        ),
        check_vma=False,
    )
```
